128 devices in a mesh: tm: 4 (over x), rows: 32 (over z, y, core).
Axes of the slice: x: 4, y: 4, z: 4, core: 2. Of those that a mesh axis runs over, the one named last changes fastest.
Arguments:
- features: bfloat16 [4, 8, 64, 96, 384], P(None, 'tm', 'rows'), may hold values from -6 to 6
- frame_counts: int32 [4], replicated, may hold values from 1 to 8, as said below
- owner_order: int32 [4], replicated, may hold values from 0 to 3, each once
- first_gain: float32 [384], replicated, may hold values from 0.1 to 1.9
- first_kernel: bfloat16 [3, 3, 3, 384, 384], replicated, may hold values from -0.0625 to 0.0625
- first_bias: float32 [384], replicated, may hold values from -3 to 3
- second_gain: float32 [384], replicated, may hold values from 0.1 to 1.9
- second_kernel: bfloat16 [3, 3, 3, 384, 384], replicated, may hold values from -0.0625 to 0.0625
- second_bias: float32 [384], replicated, may hold values from -3 to 3
Outputs:
- student_latents: bfloat16 [4, 8, 64, 96, 384], P('tm', None, None, 'rows')
The draws below stay inside these ranges and needn't reach their ends.
Inputs may be any that keep to these rules, and one draw needn't show every extreme that they name: `frame_counts`: at least one clip has exactly 8 frames. `owner_order`: each clip appears once.
All inputs are finite; a program needn't handle non-finite values.
Results may differ from the reference program's by a relative error of at most 0.008.
Values may be sent and summed in bfloat16 or wider, within the bound.
A program may use at most 128 MiB of HBM per device.

```python
import jax
import jax.numpy as jnp
from jax import lax

C = 384
W = 96
CLIPS = 4
FRAMES = 8
H = 64


def draw_frame_counts(key, part):
    first_key, second_key = jax.random.split(jax.random.fold_in(key, 17))
    counted = jax.random.randint(first_key, (CLIPS,), 1, FRAMES + 1)
    longest = jax.random.randint(second_key, (), 0, CLIPS)
    return jnp.where(jnp.arange(CLIPS) == longest, FRAMES, counted).astype(jnp.int32)


def shard_levels(own_key, dims, cuts, smallest, largest):
    level, own = 1.0, jax.random.fold_in(own_key, 6)
    for axis_at, shards_of in cuts:
        draws = jnp.exp(jax.random.uniform(jax.random.fold_in(own, axis_at), (shards_of,), jnp.float32, smallest / len(cuts), largest / len(cuts)))
        level = level * jnp.repeat(draws, dims[axis_at] // shards_of).reshape([-1 if axis == axis_at else 1 for axis in range(len(dims))])
    return level


def gaussian(rng, shape, scale, most, cuts=(), kind=jnp.bfloat16):
    values = jax.random.normal(rng, shape, jnp.float32) * scale
    if len(cuts) > 0:
        values = shard_levels(rng, shape, cuts, -0.22, 0.18) * values
    return jnp.clip(values, min=-most, max=most).astype(kind)


def setup_inputs(seed: int = 0) -> dict:
    key_of = jax.random.split(jax.random.key(seed), 10)
    return {
        "features": gaussian(key_of[0], (CLIPS, FRAMES, H, W, C), 1.0, 6.0, ((1, 4), (2, 32))),
        "frame_counts": draw_frame_counts(jax.random.fold_in(key_of[9], 71), 0),
        "owner_order": jax.random.permutation(key_of[2], CLIPS).astype(jnp.int32),
        "first_gain": jnp.clip(1.0 + 0.18 * jax.random.normal(key_of[3], (C,), jnp.float32), 0.1, 1.9),
        "first_kernel": gaussian(key_of[4], (3, 3, 3, C, C), (27 * C) ** -0.5, 0.0625),
        "first_bias": gaussian(key_of[5], (C,), 0.5, 3.0, (), jnp.float32),
        "second_gain": jnp.clip(1.0 + 0.18 * jax.random.normal(key_of[6], (C,), jnp.float32), 0.1, 1.9),
        "second_kernel": gaussian(key_of[7], (3, 3, 3, C, C), (27 * C) ** -0.5, 0.0625),
        "second_bias": gaussian(key_of[8], (C,), 0.5, 3.0, (), jnp.float32),
    }


EPSILON = 1e-06

def normalize(source, norm_gain):
    values = source.astype(jnp.float32)
    factor = lax.rsqrt(lax.optimization_barrier(jnp.mean(values * values, axis=-1, keepdims=True)) + EPSILON)
    return jax.nn.silu(values * factor * norm_gain).astype(jnp.bfloat16)

def convolve(active, kernel, addend):
    frames, height, breadth, channels = active.shape
    padded = jnp.pad(active, ((2, 0), (1, 1), (1, 1), (0, 0)))
    running = jnp.zeros((frames * height * breadth, channels), jnp.float32)
    for height_tap in range(3):
        for width_tap in range(3):
            stacked = jnp.concatenate([padded[time_tap:time_tap + frames, height_tap:height_tap + height, width_tap:width_tap + breadth] for time_tap in range(3)], axis=-1)
            stacked = stacked.reshape(-1, 3 * channels)
            running = running + jnp.dot(stacked, kernel[:, height_tap, width_tap].reshape(3 * channels, channels), preferred_element_type=jnp.float32)
    return running.reshape(frames, height, breadth, channels) + addend

def reference(features, frame_counts, owner_order, first_gain, first_kernel, first_bias, second_gain, second_kernel, second_bias):

    def one_clip(packed):
        source, frame_count = packed
        usable = (jnp.arange(FRAMES) < frame_count).astype(jnp.float32)
        hidden = convolve(normalize(source, first_gain), first_kernel, first_bias).astype(jnp.bfloat16)
        result = convolve(normalize(hidden, second_gain), second_kernel, second_bias) + source.astype(jnp.float32)
        return result.astype(jnp.bfloat16) * usable.astype(jnp.bfloat16)[:, None, None, None]
    encoded = lax.map(one_clip, (features, frame_counts))
    return jnp.take(encoded, owner_order, axis=0)
```

```python
import functools

import jax
import jax.numpy as jnp
from jax import lax
from jax.experimental import pallas as pl
from jax.experimental.pallas import tpu as pltpu
from jax.sharding import PartitionSpec as P

EPSILON = 1e-06
MESH = pl.DeviceIdType.MESH
BF16 = jnp.bfloat16
F32 = jnp.float32


def normalized(values, gain):
    factor = lax.rsqrt(jnp.mean(values * values, axis=-1, keepdims=True) + EPSILON)
    scaled = values * factor * gain
    return (scaled / (1.0 + jnp.exp(-scaled))).astype(BF16)


def kernel(
    tm,
    bands,
    send_ref,
    first_kernel,
    second_kernel,
    first_gain,
    first_bias,
    second_gain,
    second_bias,
    mask_ref,
    out_ref,
    columns,
    active,
    hidden_active,
    weights,
    middle,
    spectrum,
    products,
    weight_sems,
    a2a_send,
    a2a_recv,
    edge_send,
    edge_recv,
):
    slab = lax.axis_index("tm")
    band = lax.axis_index("rows")
    devices = tm * bands
    width, frames, height, channels = columns.shape
    pairs = frames // 2
    block = pairs * height
    own_frames = frames // tm
    own_rows = height // bands

    def peer(index):
        offset = lax.rem(index * 37, devices)
        return lax.rem(slab + offset % tm, tm), lax.rem(band + offset // tm, bands)

    barrier = pltpu.get_barrier_semaphore()

    def greet(index, carry):
        pl.semaphore_signal(barrier, inc=1, device_id=peer(index), device_id_type=MESH)
        return carry

    lax.fori_loop(1, devices, greet, 0)

    def weight_copies(layer, source):
        for q in range(3):
            for r in range(3):
                lanes = pl.ds(q * channels, channels)
                yield source.at[0, q, r], weights.at[layer, 0, r, :, lanes], weight_sems.at[layer, 0]
                yield source.at[2, q, r], weights.at[layer, 3, r, :, lanes], weight_sems.at[layer, 1]
                yield source.at[1, q, r], middle.at[layer, r, :, lanes], weight_sems.at[layer, 2]

    for layer, source in enumerate((first_kernel, second_kernel)):
        for origin, target, sem in weight_copies(layer, source):
            pltpu.make_async_copy(origin, target, sem).start()

    def transform_weights(layer):
        for slot, whole in enumerate((weights.at[layer, 0], weights.at[layer, 3], middle.at[layer])):
            pltpu.make_async_copy(whole, whole, weight_sems.at[layer, slot]).wait()
        steps = channels // 16

        def step(index, carry):
            r = index // steps
            rows = pl.ds(pl.multiple_of(index % steps * 16, 16), 16)
            early = weights[layer, 0, r, rows, :].astype(F32)
            late = weights[layer, 3, r, rows, :].astype(F32)
            half = middle[layer, r, rows, :].astype(F32) * 0.5
            outer = (early + late) * 0.5
            weights[layer, 1, r, rows, :] = (outer + half).astype(BF16)
            weights[layer, 2, r, rows, :] = (outer - half).astype(BF16)
            return carry

        lax.fori_loop(0, 3 * steps, step, 0)

    transform_weights(0)
    pl.semaphore_wait(barrier, devices - 1)

    order = (0, 2, 1)
    for c in order:
        landing = columns.at[c, pl.ds(own_frames * slab, own_frames), pl.ds(own_rows * band, own_rows)]
        pltpu.make_async_copy(send_ref.at[slab, band, c], landing, a2a_recv.at[c]).start()

        def send(index, carry):
            target = peer(index)
            pltpu.make_async_remote_copy(
                src_ref=send_ref.at[target[0], target[1], c],
                dst_ref=landing,
                send_sem=a2a_send.at[c],
                recv_sem=a2a_recv.at[c],
                device_id=target,
                device_id_type=MESH,
            ).start()
            return carry

        lax.fori_loop(1, devices, send, 0)

    transform_weights(1)

    def edge_copies(buffer, layer):
        left = pltpu.make_async_remote_copy(
            src_ref=buffer.at[1],
            dst_ref=buffer.at[width + 1],
            send_sem=edge_send.at[layer, 0],
            recv_sem=edge_recv.at[layer, 1],
            device_id=(slab, lax.rem(band + bands - 1, bands)),
            device_id_type=MESH,
        )
        right = pltpu.make_async_remote_copy(
            src_ref=buffer.at[width],
            dst_ref=buffer.at[0],
            send_sem=edge_send.at[layer, 1],
            recv_sem=edge_recv.at[layer, 0],
            device_id=(slab, lax.rem(band + 1, bands)),
            device_id_type=MESH,
        )
        return left, right

    def send_edges(buffer, layer):
        left, right = edge_copies(buffer, layer)

        @pl.when(band > 0)
        def _():
            left.start()

        @pl.when(band < bands - 1)
        def _():
            right.start()

    def take_edges(buffer, layer):
        left, right = edge_copies(buffer, layer)

        @pl.when(band > 0)
        def _():
            left.wait_send()
            right.wait_recv()

        @pl.when(band < bands - 1)
        def _():
            right.wait_send()
            left.wait_recv()

        @pl.when(band == 0)
        def _():
            buffer[0] = jnp.zeros(buffer.shape[1:], BF16)

        @pl.when(band == bands - 1)
        def _():
            buffer[width + 1] = jnp.zeros(buffer.shape[1:], BF16)

    def transform_column(buffer, c):
        def step(n, carry):
            rows = pl.ds(pl.multiple_of(n * height, height), height)
            third = buffer[c, 2 * n].astype(F32)
            fourth = buffer[c, 2 * n + 1].astype(F32)
            before = jnp.maximum(n - 1, 0)
            present = jnp.where(n > 0, 1.0, 0.0)
            first = buffer[c, 2 * before].astype(F32) * present
            second = buffer[c, 2 * before + 1].astype(F32) * present
            spectrum[0, c, rows, :] = (first - third).astype(BF16)
            spectrum[1, c, rows, :] = (second + third).astype(BF16)
            spectrum[2, c, rows, :] = (third - second).astype(BF16)
            spectrum[3, c, rows, :] = (second - fourth).astype(BF16)
            return carry

        lax.fori_loop(0, pairs, step, 0)

    def multiply(layer, outputs):
        def step(i, carry):
            left = jnp.concatenate(
                [
                    jnp.concatenate([spectrum[i, c + r] for r in range(3)], axis=1)
                    for c in outputs
                ],
                axis=0,
            )
            right = weights[layer, i].reshape(3 * channels, 3 * channels)
            product = jnp.dot(left, right, preferred_element_type=F32)
            for at, c in enumerate(outputs):
                products[i, c] = product[at * block : (at + 1) * block]
            return carry

        lax.fori_loop(0, 4, step, 0)

    row = lax.broadcasted_iota(jnp.int32, (height, channels), 0)

    def gathered(c, n):
        rows = pl.ds(pl.multiple_of(n * height, height), height)
        parts = []
        for q in range(3):
            lanes = slice(q * channels, (q + 1) * channels)
            m = [products[i, c, rows, lanes] for i in range(4)]
            parts.append((m[0] + m[1] + m[2], m[1] - m[2] - m[3]))
        for at in range(2):
            above = jnp.where(row == 0, 0.0, pltpu.roll(parts[0][at], 1, 0))
            below = jnp.where(row == height - 1, 0.0, pltpu.roll(parts[2][at], height - 1, 0))
            yield 2 * n + at, parts[1][at] + above + below

    def activate(c):
        def step(t, carry):
            active[c + 1, t] = normalized(columns[c, t].astype(F32), first_gain[...])
            return carry

        lax.fori_loop(0, frames, step, 0)

    def finish_first(c):
        def step(n, carry):
            for t, total in gathered(c, n):
                hidden = (total + first_bias[...]).astype(BF16)
                hidden_active[c + 1, t] = normalized(hidden.astype(F32), second_gain[...])
            return carry

        lax.fori_loop(0, pairs, step, 0)

    def finish_second(c):
        def step(n, carry):
            for t, total in gathered(c, n):
                result = total + second_bias[...] + columns[c, t].astype(F32)
                out_ref[c, t] = result.astype(BF16) * mask_ref[t].astype(BF16)
            return carry

        lax.fori_loop(0, pairs, step, 0)

    for c in order:
        pltpu.make_async_copy(columns.at[c], columns.at[c], a2a_recv.at[c]).wait()
        activate(c)
        if c == 2:
            send_edges(active, 0)

    transform_column(active, 1)
    transform_column(active, 2)
    transform_column(active, 3)
    multiply(0, (1,))
    take_edges(active, 0)
    transform_column(active, 0)
    transform_column(active, 4)
    multiply(0, (0, 2))
    finish_first(0)
    finish_first(2)
    send_edges(hidden_active, 1)
    finish_first(1)
    transform_column(hidden_active, 1)
    transform_column(hidden_active, 2)
    transform_column(hidden_active, 3)
    multiply(1, (1,))
    take_edges(hidden_active, 1)
    transform_column(hidden_active, 0)
    transform_column(hidden_active, 4)
    multiply(1, (0, 2))
    for c in range(3):
        finish_second(c)
    for c in order:
        for part in (send_ref.at[pl.ds(0, tm - 1), :, c], send_ref.at[tm - 1, pl.ds(0, bands - 1), c]):
            pltpu.make_async_copy(part, part, a2a_send.at[c]).wait()


def per_device(
    features,
    frame_counts,
    owner_order,
    first_gain,
    first_kernel,
    first_bias,
    second_gain,
    second_kernel,
    second_bias,
):
    tm = lax.axis_size("tm")
    bands = lax.axis_size("rows")
    clips, own_frames, own_rows, breadth, channels = features.shape
    frames, height, width = own_frames * tm, own_rows * bands, breadth // bands
    ordered = jnp.take(features, owner_order, axis=0)
    outgoing = ordered.reshape(clips, own_frames, own_rows, bands, width, channels).transpose(0, 3, 4, 1, 2, 5)
    count = frame_counts[owner_order[lax.axis_index("tm")]]
    usable = (jnp.arange(frames, dtype=jnp.int32) < count).astype(F32)
    mask = jnp.broadcast_to(usable[:, None, None], (frames, 1, channels))
    vmem = pl.BlockSpec(memory_space=pltpu.VMEM)
    anywhere = pl.BlockSpec(memory_space=pl.ANY)
    result = pl.pallas_call(
        functools.partial(kernel, tm, bands),
        out_shape=jax.ShapeDtypeStruct((width, frames, height, channels), BF16),
        in_specs=[anywhere] * 3 + [vmem] * 5,
        out_specs=vmem,
        scratch_shapes=[
            pltpu.VMEM((width, frames, height, channels), BF16),
            pltpu.VMEM((width + 2, frames, height, channels), BF16),
            pltpu.VMEM((width + 2, frames, height, channels), BF16),
            pltpu.VMEM((2, 4, 3, channels, 3 * channels), BF16),
            pltpu.VMEM((2, 3, channels, 3 * channels), BF16),
            pltpu.VMEM((4, width + 2, frames // 2 * height, channels), BF16),
            pltpu.VMEM((4, width, frames // 2 * height, 3 * channels), F32),
            pltpu.SemaphoreType.DMA((2, 3)),
            pltpu.SemaphoreType.DMA((3,)),
            pltpu.SemaphoreType.DMA((3,)),
            pltpu.SemaphoreType.DMA((2, 2)),
            pltpu.SemaphoreType.DMA((2, 2)),
        ],
        compiler_params=pltpu.CompilerParams(
            collective_id=0, has_side_effects=True, vmem_limit_bytes=62 * 2**20
        ),
        name="residual_block",
    )(
        outgoing,
        first_kernel,
        second_kernel,
        first_gain[None],
        first_bias[None],
        second_gain[None],
        second_bias[None],
        mask,
    )
    return result.transpose(1, 2, 0, 3)[None]


def solution(mesh):
    placed = (P(None, "tm", "rows", None, None), P(), P(), P(), P(), P(), P(), P(), P())
    return jax.shard_map(
        per_device,
        mesh=mesh,
        in_specs=placed,
        out_specs=P("tm", None, None, "rows", None),
        check_vma=False,
    )
```
